32 devices in a mesh: engine: 2 (over y), ep: 16 (over z, x, core).
Axes of the slice: x: 2, y: 2, z: 4, core: 2. Of those that a mesh axis runs over, the one named last changes fastest.
Arguments:
- tokens: bfloat16 [2, 256, 4096], P(None, ('engine', 'ep')), may hold values from -6 to 6
- route_ids: int32 [2, 256, 8], P(None, ('engine', 'ep')), may hold values from 0 to 15, all different within a row; in each aligned block of 8 rows (0 to 7, 8 to 15, ..., all dimensions but the last counted through in order) at most 4 rows name the same one
- route_weights: float32 [2, 256, 8], P(None, ('engine', 'ep')), may hold values from 0.05 to 1
- placement: int32 [16], replicated, may hold values from 0 to 15, each once
- expert_in: bfloat16 [16, 2, 4096, 1536], P(None, None, ('engine', 'ep')), may hold values from -0.09375 to 0.09375
- expert_down: bfloat16 [16, 1536, 4096], P(None, None, ('engine', 'ep')), may hold values from -0.15625 to 0.15625
Outputs:
- combined: bfloat16 [2, 256, 4096], P(None, ('engine', 'ep'))
- in_scales: float32 [16, 2, 1536], P('ep', None, 'engine')
- out_scales: float32 [16, 4096], P('ep', 'engine')
The draws below stay inside these ranges and needn't reach their ends.
Inputs may be any that keep to these rules, and one draw needn't show every extreme that they name: `route_ids`: within the rows of one device in one step no expert is named more than 4 times, a bound that some block reaches. `placement`: each slot holds exactly one expert.
All inputs are finite; a program needn't handle non-finite values.
Results may differ from the reference program's by a relative error of at most 0.0057.
Values may be sent and summed in bfloat16 or wider, within the bound.
No kernel may reach another device: no remote copies, remote signals or barrier semaphores. Data moves between devices by JAX's collectives and lax.ppermute only.
A program may use at most 128 MiB of HBM per device.

```python
import math
import jax
import jax.numpy as jnp
import numpy as np
from jax import lax

D = 4096
FF = 1536
TOP = 8
STEPS = 2
TOK_DEV = 8
EXPERTS = 16
MOST = 4
TOKENS = 256


def shard_levels(own_key, extent, pieces, low, top_value):
    def one(position, parts):
        heights = jax.random.uniform(jax.random.fold_in(jax.random.fold_in(own_key, 6), position), (parts,), jnp.float32, low / len(pieces), top_value / len(pieces))
        return jnp.repeat(jnp.exp(heights), extent[position] // parts).reshape((-1,) + (1,) * (len(extent) - position - 1))

    level = one(*pieces[0])
    for cut in pieces[1:]:
        level = level * one(*cut)
    return level


def shared_out(key, own, number, rows, number_of, top, bound, lean):
    sequence = jax.random.permutation(key, number_of)
    heavy_load, common = load_shares(number_of, rows * top, bound, lean, True), load_shares(number_of, rows * top, bound, lean, False)
    places = jnp.arange(number_of)

    def named(lengths, turn):
        used = int((lengths > 0).sum())
        fixed = max(1, used // 4)
        passed = fixed + (places - fixed + turn * (used - fixed)) % max(1, number_of - fixed)
        return jnp.zeros((number_of,), jnp.int32).at[sequence[jnp.where(places < fixed, places, passed)]].set(jnp.asarray(lengths, jnp.int32))

    lengths = jnp.where(number % 4 == 0, named(heavy_load, number // 4), named(common, number - number // 4 - 1))
    mixed = jax.random.permutation(jax.random.fold_in(own, 3), number_of)
    donor, taker = mixed[0:number_of // 2 * 2:2], mixed[1:number_of // 2 * 2:2]
    margin = jnp.minimum(lengths[donor] - 1, bound - lengths[taker]) // 2
    margin = jnp.where((donor == sequence[0]) | (taker == sequence[0]) | (lengths[taker] == 0), 0, jnp.maximum(margin, 0))
    passed = jax.random.randint(jax.random.fold_in(own, 4), (number_of // 2,), 0, 1 << 20) % (margin + 1)
    lengths = lengths.at[donor].add(-passed).at[taker].add(passed)
    labels = jnp.searchsorted(jnp.cumsum(lengths), jnp.arange(rows * top), side="right").astype(jnp.int32)
    table = labels.reshape(top, rows).T
    table = table[jax.random.permutation(jax.random.fold_in(own, 1), rows)]
    turn = jax.random.randint(jax.random.fold_in(own, 2), (rows, 1), 0, top)
    return jnp.take_along_axis(table, (jnp.arange(top)[None, :] + turn) % top, axis=1)


def load_shares(count, total, bound, skew, full):
    portions = [(1 << 20) // math.isqrt(grade ** skew) + 1 for grade in range(1, count + 1)]
    largest = bound if full else min(bound, max(-(-total // count), total * portions[0] // sum(portions)))
    least = 1 if total - largest >= count - 1 else 0
    holding, surplus = [largest] + [least] * (count - 1), total - largest - least * (count - 1)
    while surplus > 0:
        free = [i for i in range(1, count) if holding[i] < largest] or [i for i in range(1, count) if holding[i] < bound]
        pool, budget = sum([portions[i] for i in free]), surplus
        for i in free:
            more = min(bound - holding[i], max(1, budget * portions[i] // pool), surplus)
            holding[i] = holding[i] + more
            surplus = surplus - more
    return np.array(holding)


def normal_values(stream_key, dims, scale, most, split=(), kind=jnp.bfloat16):
    loudness = shard_levels(stream_key, dims, split, -0.22, 0.18) if split else 1.0
    values = jax.random.normal(stream_key, dims, jnp.float32) * scale * loudness
    return jnp.minimum(jnp.maximum(values, -most), most).astype(kind)


def setup_inputs(seed: int = 0) -> dict:
    key_of = jax.random.split(jax.random.key(seed), 7)
    tokens = normal_values(key_of[0], (STEPS, TOKENS, D), 1.0, 6.0, ((1, 32),))
    route_ids_keys = jax.random.split(jax.random.fold_in(key_of[1], 1), STEPS * TOKENS // TOK_DEV)
    route_ids_turns = jax.random.permutation(jax.random.fold_in(key_of[1], 3), STEPS * TOKENS // TOK_DEV)
    route_ids = jax.vmap(lambda own, number: shared_out(jax.random.fold_in(key_of[1], 2), own, number, TOK_DEV, EXPERTS, TOP, MOST, 1))(route_ids_keys, route_ids_turns).reshape((STEPS, TOKENS, TOP))
    route_weights = jnp.clip(0.05 + 0.95 * jax.random.uniform(key_of[2], (STEPS, TOKENS, TOP), jnp.float32) ** shard_levels(key_of[2], (STEPS, TOKENS, TOP), ((1, 32),), -0.2, 0.2), 0.05, 1.0)
    placement = jax.random.permutation(key_of[3], EXPERTS).astype(jnp.int32)
    expert_in = normal_values(key_of[4], (EXPERTS, 2, D, FF), D ** -0.5, 0.09375, ((2, 32),))
    expert_down = normal_values(key_of[5], (EXPERTS, FF, D), FF ** -0.5, 0.15625, ((2, 32),))
    return {"tokens": tokens, "route_ids": route_ids, "route_weights": route_weights, "placement": placement, "expert_in": expert_in, "expert_down": expert_down}


EPSILON = 1e-6
quant_levels = 31.0


def reference(tokens, route_ids, route_weights, placement, expert_in, expert_down):
    experts = expert_in.shape[0]
    row_room = (TOKENS // TOK_DEV) * MOST
    positions = jnp.arange(row_room, dtype=jnp.int32)

    def one_expert(running, expert_id):
        weights_in = expert_in[expert_id].astype(jnp.float32)
        weights_down = expert_down[expert_id].astype(jnp.float32)
        scale_in = (jnp.max(jnp.abs(weights_in), axis=1) + EPSILON) / quant_levels
        scale_out = (jnp.max(jnp.abs(weights_down), axis=0) + EPSILON) / quant_levels
        quant_in = jnp.floor(weights_in / scale_in[:, None, :] + 0.5).astype(jnp.bfloat16)
        quant_down = jnp.floor(weights_down / scale_out[None, :] + 0.5).astype(jnp.bfloat16)
        updated = []
        for step_index in range(STEPS):
            matched = route_ids[step_index] == expert_id
            weight_sum = jnp.sum(jnp.where(matched, route_weights[step_index], 0.0), axis=1)
            chosen = jnp.any(matched, axis=1)
            row_ids = jnp.nonzero(chosen, size=row_room, fill_value=0)[0].astype(jnp.int32)
            usable = positions < jnp.sum(chosen.astype(jnp.int32))
            picked = tokens[step_index][row_ids]
            gate_part = jnp.dot(picked, quant_in[0], preferred_element_type=jnp.float32) * scale_in[0]
            up_part = jnp.dot(picked, quant_in[1], preferred_element_type=jnp.float32) * scale_in[1]
            hidden = (jax.nn.silu(gate_part) * up_part).astype(jnp.bfloat16)
            result = (jnp.dot(hidden, quant_down, preferred_element_type=jnp.float32) * scale_out).astype(jnp.bfloat16)
            weight = jnp.where(usable, weight_sum[row_ids], 0.0)
            updated.append(running[step_index].at[row_ids].add(result.astype(jnp.float32) * weight[:, None]))
        return jnp.stack(updated), (scale_in, scale_out)

    initial = jnp.zeros((STEPS, TOKENS, D), jnp.float32)
    summed, scales = lax.scan(one_expert, initial, jnp.arange(experts, dtype=jnp.int32))
    scales_in, scales_out = scales
    slot_in = jnp.zeros_like(scales_in).at[placement].set(scales_in)
    slot_out = jnp.zeros_like(scales_out).at[placement].set(scales_out)
    return summed.astype(jnp.bfloat16), slot_in, slot_out
```

```python
from functools import partial

import jax
import jax.numpy as jnp
from jax import lax
from jax.experimental import pallas as pl
from jax.experimental.pallas import tpu as pltpu
from jax.sharding import Mesh, PartitionSpec as P

EPSILON = 1e-06
quant_levels = 31.0
LANES = 128


GROUP = ("engine", "lo")
EVERY = ("engine", "hi", "lo")
SLOTS = ("hi", "lo")


def to_scale(largest):
    return (largest.astype(jnp.float32) + EPSILON) / quant_levels


def quantize(values, inverse):
    return jnp.floor(values.astype(jnp.float32) * inverse + 0.5).astype(jnp.bfloat16)


def exchange(values, axes):
    return lax.all_to_all(values, axes, 0, 0, tiled=True)


def project_body(count, x_ref, inv_ref, *refs):
    piece_refs, out_ref = refs[:count], refs[count]
    inverse = inv_ref[0]
    total = None
    for first in range(0, count, 2):
        block = jnp.concatenate(
            [quantize(ref[0], inverse) for ref in piece_refs[first : first + 2]], axis=0
        )
        depth = piece_refs[first].shape[1]
        columns = x_ref[:, first * depth : first * depth + block.shape[0]]
        part = jnp.dot(columns, block, preferred_element_type=jnp.float32)
        total = part if total is None else total + part
    out_ref[0] = total.astype(out_ref.dtype)


def project(rows, pieces, inverse):
    matrices, depth, width = pieces[0].shape
    row_count = rows.shape[0]
    tile = 2 * LANES
    count = len(pieces)
    return pl.pallas_call(
        partial(project_body, count),
        out_shape=jax.ShapeDtypeStruct((matrices, row_count, width), jnp.bfloat16),
        grid=(matrices, width // tile),
        in_specs=[
            pl.BlockSpec(rows.shape, lambda m, j: (0, 0)),
            pl.BlockSpec((1, 1, tile), lambda m, j: (m, 0, j)),
        ]
        + [pl.BlockSpec((1, depth, tile), lambda m, j: (m, 0, j))] * count,
        out_specs=pl.BlockSpec((1, row_count, tile), lambda m, j: (m, 0, j)),
        cost_estimate=pl.CostEstimate(
            flops=2 * row_count * count * depth * matrices * width,
            bytes_accessed=2 * count * depth * matrices * width,
            transcendentals=0,
        ),
    )(rows, inverse[:, None, :], *pieces)


def descend_body(hidden_ref, quant_ref, scale_ref, out_ref):
    pair = jnp.concatenate([quant_ref[n] for n in range(quant_ref.shape[0])], axis=1)
    total = jnp.dot(hidden_ref[...], pair, preferred_element_type=jnp.float32)
    out_ref[...] = (total * scale_ref[...]).astype(out_ref.dtype)


def descend(hidden, quant, scale):
    sources, units, width = quant.shape
    row_count = hidden.shape[0]
    if width % LANES or sources % 2:
        total = jnp.einsum("rj,sjd->rsd", hidden, quant, preferred_element_type=jnp.float32)
        return (total * scale[None]).astype(jnp.bfloat16).reshape(row_count, sources * width)
    tile = 2 * width
    return pl.pallas_call(
        descend_body,
        out_shape=jax.ShapeDtypeStruct((row_count, sources * width), jnp.bfloat16),
        grid=(sources // 2,),
        in_specs=[
            pl.BlockSpec(hidden.shape, lambda n: (0, 0)),
            pl.BlockSpec((2, units, width), lambda n: (n, 0, 0)),
            pl.BlockSpec((1, tile), lambda n: (0, n)),
        ],
        out_specs=pl.BlockSpec((row_count, tile), lambda n: (0, n)),
        cost_estimate=pl.CostEstimate(
            flops=2 * row_count * units * sources * width,
            bytes_accessed=2 * units * sources * width,
            transcendentals=0,
        ),
    )(hidden, quant, scale.reshape(1, sources * width))


def shards(tokens, route_ids, route_weights, placement, expert_in, expert_down):
    experts, matrices, depth, units = expert_in.shape
    steps, row_count, model = tokens.shape
    features = expert_down.shape[2]
    engines, copies, lows = (lax.axis_size(axis) for axis in EVERY)
    high = lax.axis_index("hi")
    me = lax.axis_index("engine") * lows + lax.axis_index("lo")
    numbers = jnp.arange(experts, dtype=jnp.int32)
    capacity = max(2, (row_count * route_ids.shape[2] + experts - 1) // experts)
    slots = jnp.arange(capacity, dtype=jnp.int32)
    lanes = steps * capacity

    aligned = depth % LANES == 0 and units % (2 * LANES) == 0
    pieces = []
    for shift in range(experts if aligned else 0):
        piece = lax.dynamic_index_in_dim(expert_in, me ^ shift, 0, keepdims=False)
        if shift:
            piece = lax.ppermute(piece, GROUP, [(n, n ^ shift) for n in range(experts)])
        pieces.append(piece)

    largest = jnp.max(jnp.abs(expert_in), axis=2)
    own = jnp.max(exchange(largest, GROUP).reshape(experts, matrices, units), axis=0)
    for shift in range(1, copies):
        far = lax.ppermute(own if shift == 1 else far, "hi", [(n, (n + 1) % copies) for n in range(copies)])
        own = jnp.maximum(own, far)
    scale_in = to_scale(own)

    holders = jnp.sum(jnp.where(placement[None, :] == numbers[:, None], numbers[None, :], 0), axis=1)
    by_slot = jnp.take(largest, holders, axis=0).reshape(experts, matrices, engines, units // engines)
    by_slot = jnp.transpose(by_slot, (2, 0, 1, 3)).reshape(engines * experts, matrices, units // engines)
    in_scales = to_scale(jnp.max(exchange(by_slot, EVERY), axis=0, keepdims=True))

    scale_down = to_scale(jnp.max(jnp.abs(expert_down), axis=1))
    quant_down = quantize(expert_down, 1.0 / scale_down[:, None, :])
    out_scales = exchange(jnp.take(scale_down, holders, axis=0), SLOTS).reshape(1, -1)
    held_scale = exchange(scale_down, GROUP)

    named = route_ids[:, :, :, None] == numbers
    chosen = jnp.any(named, axis=2)
    places = jnp.arange(row_count, dtype=jnp.int32)
    earlier = places[:, None] > places[None, :]
    rank = jnp.sum(
        (earlier[None, :, :, None] & chosen[:, None, :, :]).astype(jnp.int32), axis=2
    )
    placed = chosen[..., None] & (rank[..., None] == slots)
    share = jnp.sum(jnp.where(named, route_weights[..., None], 0.0), axis=2)
    same = jnp.eye(steps, dtype=jnp.bool_)
    taken = jnp.transpose(placed, (2, 0, 3, 1))[:, :, :, None, :] & same[None, :, None, :, None]
    taken = taken.reshape(experts * lanes, steps * row_count)
    packed = jnp.dot(
        taken.astype(jnp.bfloat16),
        tokens.reshape(steps * row_count, model),
        preferred_element_type=jnp.float32,
    ).astype(jnp.bfloat16)
    packed = packed.reshape(engines, lows, lanes, engines, copies, lows * depth)
    packed = jnp.transpose(packed, (0, 4, 1, 2, 3, 5))
    packed = packed.reshape(engines * copies * lows, lanes, engines * lows * depth)
    rows = exchange(packed, EVERY).reshape(-1, experts, depth)

    if aligned:
        rows = jnp.take(rows, me ^ numbers, axis=1).reshape(-1, experts * depth)
        partial_sums = project(rows, pieces, 1.0 / scale_in)
    else:
        held_in = quantize(exchange(expert_in, GROUP), 1.0 / scale_in[:, None, :])
        partial_sums = jnp.einsum(
            "rnd,nmdj->mrj", rows, held_in, preferred_element_type=jnp.float32
        ).astype(jnp.bfloat16)
    total_rows = rows.shape[0]
    each = total_rows // copies
    partial_sums = partial_sums.reshape(matrices, copies, each, units)
    summed = lax.dynamic_index_in_dim(partial_sums, high, 1, keepdims=False).astype(jnp.float32)
    for shift in range(1, copies):
        sent = lax.dynamic_index_in_dim(partial_sums, (high + shift) % copies, 1, keepdims=False)
        sent = lax.ppermute(sent, "hi", [(n, (n + shift) % copies) for n in range(copies)])
        summed = summed + sent.astype(jnp.float32)
    summed = summed * scale_in[:, None, :]
    hidden = (jax.nn.silu(summed[0]) * summed[1]).astype(jnp.bfloat16)
    gathered = [hidden]
    for shift in range(1, copies):
        gathered.append(lax.ppermute(hidden, "hi", [(n, (n + shift) % copies) for n in range(copies)]))
    order = (high - jnp.arange(copies, dtype=jnp.int32)) % copies
    hidden = jnp.take(jnp.stack(gathered), order, axis=0).reshape(total_rows, units)

    held_down = exchange(quant_down, GROUP)
    outcome = descend(hidden, held_down, held_scale)
    returned = exchange(outcome.reshape(-1, lanes, experts * features), EVERY)
    mixing = jnp.where(placed, share[..., None], 0.0)
    mixing = jnp.where(same[:, None, None, :, None], mixing[:, :, :, None, :], 0.0)
    mixing = mixing.reshape(steps * row_count, experts * lanes)
    returned = returned.reshape(engines, copies, lows * lanes, experts * features)
    returned = jnp.transpose(returned, (1, 0, 2, 3)).reshape(copies, experts * lanes, experts * features)
    merged = jnp.einsum(
        "rn,hnd->rhd", mixing, returned.astype(jnp.float32), precision=lax.Precision.HIGHEST
    )
    merged = merged.reshape(steps, row_count, copies, engines, lows * features)
    merged = jnp.transpose(merged, (0, 1, 3, 2, 4)).reshape(steps, row_count, model)
    return merged.astype(jnp.bfloat16), in_scales, out_scales


def solution(mesh):
    engines = mesh.shape["engine"]
    fine = Mesh(mesh.devices.reshape(engines, engines, -1), EVERY)
    ep = ("hi", "lo")
    placed = (
        P(None, EVERY, None),
        P(None, EVERY, None),
        P(None, EVERY, None),
        P(),
        P(None, None, EVERY, None),
        P(None, None, EVERY),
    )
    return jax.shard_map(
        shards,
        mesh=fine,
        in_specs=placed,
        out_specs=(P(None, EVERY, None), P(ep, None, "engine"), P(ep, "engine")),
        check_vma=False,
    )
```

```python
from functools import partial

import jax
import jax.numpy as jnp
import numpy as np
from jax import lax
from jax.experimental import pallas as pl
from jax.experimental.pallas import tpu as pltpu
from jax.sharding import Mesh, PartitionSpec as P

EPSILON = 1e-06
quant_levels = 31.0
LANES = 128


GROUP = ("engine", "lo")
EVERY = ("engine", "hi", "lo")


def to_scale(largest):
    return (largest.astype(jnp.float32) + EPSILON) / quant_levels


def quantize(values, inverse):
    return jnp.floor(values.astype(jnp.float32) * inverse + 0.5).astype(jnp.bfloat16)


def column_cuts(width):
    tiles = width // (2 * LANES)
    edges = [0, (tiles + 1) // 2 * 2 * LANES, width]
    return [(low, top) for low, top in zip(edges, edges[1:]) if low < top]


def parity(number):
    return bin(number >> 1).count("1") % 2


def exchange(values, axes):
    return lax.all_to_all(values, axes, 0, 0, tiled=True)


def project_body(count, x_ref, inv_ref, *refs):
    piece_refs, kept_ref, sent_ref = refs[:count], refs[count], refs[count + 1]
    inverse = inv_ref[0]
    total = None
    for first in range(0, count, 2):
        block = jnp.concatenate(
            [quantize(ref[0], inverse) for ref in piece_refs[first : first + 2]], axis=0
        )
        depth = piece_refs[first].shape[1]
        columns = x_ref[:, first * depth : first * depth + block.shape[0]]
        part = jnp.dot(columns, block, preferred_element_type=jnp.float32)
        total = part if total is None else total + part
    each = kept_ref.shape[1]
    kept_ref[0] = total[:each]
    sent_ref[0] = total[each:].astype(sent_ref.dtype)


def project(rows, pieces, inverse, each):
    matrices, depth, width = pieces[0].shape
    row_count = rows.shape[0]
    tile = 2 * LANES
    count = len(pieces)
    return pl.pallas_call(
        partial(project_body, count),
        out_shape=(
            jax.ShapeDtypeStruct((matrices, each, width), jnp.float32),
            jax.ShapeDtypeStruct((matrices, row_count - each, width), jnp.bfloat16),
        ),
        grid=(matrices, width // tile),
        in_specs=[
            pl.BlockSpec(rows.shape, lambda m, j: (0, 0)),
            pl.BlockSpec((1, 1, tile), lambda m, j: (m, 0, j)),
        ]
        + [pl.BlockSpec((1, depth, tile), lambda m, j: (m, 0, j))] * count,
        out_specs=(
            pl.BlockSpec((1, each, tile), lambda m, j: (m, 0, j)),
            pl.BlockSpec((1, row_count - each, tile), lambda m, j: (m, 0, j)),
        ),
        cost_estimate=pl.CostEstimate(
            flops=2 * row_count * count * depth * matrices * width,
            bytes_accessed=2 * count * depth * matrices * width,
            transcendentals=0,
        ),
    )(rows, inverse[:, None, :], *pieces)


def descend_body(count, order_ref, hidden_ref, scale_ref, *refs):
    piece_refs, out_ref = refs[:count], refs[count]
    width = piece_refs[0].shape[1]
    hidden = hidden_ref[...]
    for first in range(0, count, 2):
        pair = jnp.concatenate([ref[...] for ref in piece_refs[first : first + 2]], axis=1)
        total = jnp.dot(hidden, pair, preferred_element_type=jnp.float32)
        for n in range(first, min(first + 2, count)):
            start = pl.multiple_of(order_ref[n] * width, width)
            part = total[:, (n - first) * width : (n - first + 1) * width]
            part = part * scale_ref[n]
            out_ref[:, pl.ds(start, width)] = part.astype(out_ref.dtype)


def descend(hidden, pieces, scale, order):
    count = len(pieces)
    units, width = pieces[0].shape
    row_count = hidden.shape[0]
    return pl.pallas_call(
        partial(descend_body, count),
        out_shape=jax.ShapeDtypeStruct((row_count, count * width), jnp.bfloat16),
        in_specs=[pl.BlockSpec(memory_space=pltpu.SMEM)]
        + [pl.BlockSpec(memory_space=pltpu.VMEM)] * (2 + count),
        out_specs=pl.BlockSpec(memory_space=pltpu.VMEM),
        cost_estimate=pl.CostEstimate(
            flops=2 * row_count * units * count * width,
            bytes_accessed=2 * units * count * width,
            transcendentals=0,
        ),
    )(order, hidden, scale[:, None, :], *pieces)


def layer(tokens, route_ids, route_weights, placement, expert_in, expert_down):
    experts, matrices, depth, units = expert_in.shape
    steps, row_count, model = tokens.shape
    features = expert_down.shape[2]
    engines, copies, lows = (lax.axis_size(axis) for axis in EVERY)
    devices = engines * copies * lows
    engine, high = lax.axis_index("engine"), lax.axis_index("hi")
    me = engine * lows + lax.axis_index("lo")
    numbers = jnp.arange(experts, dtype=jnp.int32)
    capacity = max(2, (row_count * route_ids.shape[2] + experts - 1) // experts)
    slots = jnp.arange(capacity, dtype=jnp.int32)
    lanes = steps * capacity
    aligned = depth % LANES == 0 and features % LANES == 0 and units % (2 * LANES) == 0
    pairs = [[(n, n ^ shift) for n in range(experts)] for shift in range(experts)]
    turn = [[(n, (n + shift) % copies) for n in range(copies)] for shift in range(copies)]

    cuts = column_cuts(units) if aligned else []

    def move(number, held):
        low, top = cuts[number]
        pieces = []
        for shift in range(experts):
            piece = lax.dynamic_slice(
                held, (me ^ shift, 0, 0, low), (1, matrices, depth, top - low)
            )[0]
            if shift:
                piece = lax.ppermute(piece, GROUP, pairs[shift])
            pieces.append(piece)
        return pieces

    chunks = [move(0, expert_in)] if aligned else []

    largest_in = jnp.max(jnp.abs(expert_in), axis=2)
    largest_down = jnp.max(jnp.abs(expert_down), axis=1)
    holders = jnp.sum(
        jnp.where(placement[None, :] == numbers[:, None], numbers[None, :], 0), axis=1
    )
    by_slot = (holders[:, None] == numbers[None, :]).astype(jnp.bfloat16)

    def sort_slots(values):
        return jnp.dot(by_slot, values, preferred_element_type=jnp.float32).astype(jnp.bfloat16)

    slot_in = sort_slots(largest_in.reshape(experts, -1))
    slot_in = slot_in.reshape(experts, matrices, engines, units // engines)
    slot_in = jnp.transpose(slot_in, (2, 0, 1, 3)).reshape(engines, experts, -1)
    slot_down = jnp.broadcast_to(sort_slots(largest_down), (engines, experts, features))
    slot_part = jnp.concatenate([slot_in, slot_down], axis=2)
    slot_part = slot_part.reshape(engines, copies, lows, -1)
    own_part = jnp.concatenate([largest_in.reshape(experts, -1), largest_down], axis=1)
    own_part = own_part.reshape(engines, 1, lows, -1)
    own_part = jnp.broadcast_to(own_part, (engines, copies, lows, own_part.shape[-1]))

    named = route_ids[:, :, :, None] == numbers
    chosen = jnp.any(named, axis=2)
    places = jnp.arange(row_count, dtype=jnp.int32)
    earlier = places[:, None] > places[None, :]
    rank = jnp.sum((earlier[None, :, :, None] & chosen[:, None, :, :]).astype(jnp.int32), axis=2)
    placed = chosen[..., None] & (rank[..., None] == slots)
    share = jnp.sum(jnp.where(named, route_weights[..., None], 0.0), axis=2)
    same = jnp.eye(steps, dtype=jnp.bool_)
    taken = jnp.transpose(placed, (2, 0, 3, 1))[:, :, :, None, :] & same[None, :, None, :, None]
    taken = taken.reshape(experts * lanes, steps * row_count)
    packed = jnp.dot(
        taken.astype(jnp.bfloat16),
        tokens.reshape(steps * row_count, model),
        preferred_element_type=jnp.float32,
    ).astype(jnp.bfloat16)
    packed = packed.reshape(engines, lows, lanes, engines, copies, lows * depth)
    packed = jnp.transpose(packed, (0, 4, 1, 2, 3, 5))
    packed = packed.reshape(engines, copies, lows, lanes * experts * depth)
    extra = jnp.concatenate([own_part, slot_part], axis=3)
    extra_count = extra.shape[3]
    wide = experts * depth
    extra_rows = -(-extra_count // wide)
    extra = jnp.pad(extra, ((0, 0), (0, 0), (0, 0), (0, extra_rows * wide - extra_count)))
    parcel = jnp.concatenate([packed, extra], axis=3).reshape(devices, lanes + extra_rows, wide)
    if aligned:
        parcel, expert_in = lax.optimization_barrier((parcel, expert_in))
    arrived = exchange(parcel, EVERY)

    for number in range(1, len(cuts)):
        chunks.append(move(number, expert_in))

    rows = arrived[:, :lanes].reshape(devices, lanes, experts, depth)
    extra = arrived[:, lanes:].reshape(devices, extra_rows * wide)
    count_in = matrices * units
    scale_in = to_scale(jnp.max(extra[:, :count_in], axis=0)).reshape(matrices, units)
    held_scale = extra[:, count_in : count_in + features].reshape(engines, copies, lows, features)
    held_scale = to_scale(lax.dynamic_index_in_dim(held_scale, high, 1, keepdims=False))
    held_scale = held_scale.reshape(experts, features)
    first = count_in + features
    in_scales = to_scale(jnp.max(extra[:, first : first + count_in // engines], axis=0))
    in_scales = in_scales.reshape(1, matrices, units // engines)
    first = first + count_in // engines
    out_scales = extra[:, first : first + features].reshape(engines, copies * lows * features)
    out_scales = to_scale(lax.dynamic_index_in_dim(out_scales, engine, 0, keepdims=True))
    total_rows = devices * lanes
    each = total_rows // copies
    turns = (high + jnp.arange(copies, dtype=jnp.int32)) % copies
    rows = jnp.take(rows.reshape(copies, each, experts, depth), turns, axis=0)
    scale_down = to_scale(largest_down)
    quant_down = quantize(expert_down, 1.0 / scale_down[:, None, :])

    if aligned:
        rows = jnp.take(rows, me ^ numbers, axis=2).reshape(total_rows, experts * depth)
        sums = [
            project(rows, pieces, 1.0 / scale_in[:, low:top], each)
            for (low, top), pieces in zip(cuts, chunks, strict=True)
        ]
    else:
        cuts = [(0, units)]
        held_in = quantize(exchange(expert_in, GROUP), 1.0 / scale_in[:, None, :])
        total = jnp.einsum(
            "rnd,nmdj->mrj",
            rows.reshape(total_rows, experts, depth),
            held_in,
            preferred_element_type=jnp.float32,
        )
        sums = [(total[:, :each], total[:, each:].astype(jnp.bfloat16))]
    swapped = []
    for summed, sent in sums:
        for shift in range(1, copies):
            near = sent[:, (shift - 1) * each : shift * each]
            near = lax.ppermute(near, "hi", turn[shift])
            summed = summed + near.astype(jnp.float32)
        swapped.append(summed)

    halves = [[shift for shift in range(experts) if parity(shift) == half] for half in range(2)]
    held_down = []
    for half in range(2 if aligned else 0):
        pieces = []
        for shift in halves[half]:
            piece = lax.dynamic_index_in_dim(quant_down, me ^ shift, 0, keepdims=False)
            if shift:
                piece = lax.ppermute(piece, GROUP, pairs[shift])
            pieces.append(piece)
        held_down.append(pieces)

    hidden = []
    for (low, top), summed in zip(cuts, swapped, strict=True):
        summed = summed * scale_in[:, None, low:top]
        hidden.append((jax.nn.silu(summed[0]) * summed[1]).astype(jnp.bfloat16))
    hidden = jnp.concatenate(hidden, axis=1)
    gathered = [hidden]
    for shift in range(1, copies):
        gathered.append(lax.ppermute(hidden, "hi", turn[shift]))
    order = (high - jnp.arange(copies, dtype=jnp.int32)) % copies
    hidden = jnp.take(jnp.stack(gathered), order, axis=0).reshape(total_rows, units)

    mixing = jnp.where(placed, share[..., None], 0.0)
    mixing = jnp.where(same[:, None, None, :, None], mixing[:, :, :, None, :], 0.0)
    mixing = mixing.reshape(steps * row_count, experts * lanes)

    def by_copy(values):
        values = values.reshape(engines, copies, lows, lanes, -1)
        return jnp.transpose(values, (1, 0, 2, 3, 4)).reshape(copies, experts * lanes, -1)

    def merge(values):
        values = values.astype(jnp.float32)
        return jnp.einsum("rn,hnd->rhd", mixing, values, precision=lax.Precision.HIGHEST)

    if aligned:
        returned = []
        for half, pieces in enumerate(held_down):
            sources = me ^ jnp.asarray(halves[half], jnp.int32)
            scales = jnp.take(held_scale, sources, axis=0)
            outcome = descend(hidden, pieces, scales, sources // 2 // 2 * 2 + sources % 2)
            width = len(pieces) * features
            returned.append(by_copy(exchange(outcome.reshape(devices, lanes, width), EVERY)))
        odd = np.repeat([parity(n) for n in range(experts)], lanes)[None, :, None]
        merged = [merge(jnp.where(odd == half, *returned)) for half in range(2)]
        merged = jnp.stack(merged, axis=2).reshape(steps * row_count, copies, experts, features)
        blocks = [n for half in range(2) for n in range(experts) if parity(n) == half]
        merged = jnp.take(merged, np.argsort(np.array(blocks)), axis=2)
    else:
        total = jnp.einsum(
            "rj,njd->rnd",
            hidden,
            exchange(quant_down, GROUP),
            preferred_element_type=jnp.float32,
        )
        outcome = (total * held_scale[None]).astype(jnp.bfloat16)
        merged = merge(by_copy(exchange(outcome.reshape(devices, lanes, -1), EVERY)))
    merged = merged.reshape(steps, row_count, copies, engines, lows * features)
    merged = jnp.transpose(merged, (0, 1, 3, 2, 4)).reshape(steps, row_count, model)
    return merged.astype(jnp.bfloat16), in_scales, out_scales


def solution(mesh):
    engines = mesh.shape["engine"]
    fine = Mesh(mesh.devices.reshape(engines, engines, -1), EVERY)
    ep = ("hi", "lo")
    placed = (
        P(None, EVERY, None),
        P(None, EVERY, None),
        P(None, EVERY, None),
        P(),
        P(None, None, EVERY, None),
        P(None, None, EVERY),
    )
    return jax.shard_map(
        layer,
        mesh=fine,
        in_specs=placed,
        out_specs=(P(None, EVERY, None), P(ep, None, "engine"), P(ep, "engine")),
        check_vma=False,
    )
```
